32 devices in a mesh: row: 8 (over y, x, core), col: 4 (over z).
Axes of the slice: x: 2, y: 2, z: 4, core: 2. Of those that a mesh axis runs over, the one named last changes fastest.
Arguments:
- tokens: bfloat16 [8192, 1536], P(('row', 'col')), may hold values from -6 to 6
- segment_ids: int32 [8192], P('row'), may hold values from 0 to 31, as said below
- positions: int32 [8192], P('row'), may hold values from 0 to 1023, as said below
- norm_attn: float32 [2, 1536], replicated, may hold values from 0.5 to 1.5
- qkv_weight: bfloat16 [2, 1536, 3072], P(None, 'row', 'col'), may hold values from -0.15625 to 0.15625
- out_weight: bfloat16 [2, 1536, 1536], P(None, 'col', 'row'), may hold values from -0.625 to 0.625
- norm_mlp: float32 [2, 1536], replicated, may hold values from 0.5 to 1.5
- gate_up_weight: bfloat16 [2, 1536, 2, 4096], P(None, 'row', None, 'col'), may hold values from -0.15625 to 0.15625
- down_weight: bfloat16 [2, 1536, 4096], P(None, 'row', 'col'), may hold values from -0.09375 to 0.09375
- cotangent: bfloat16 [8192, 1536], P(('row', 'col')), may hold values from -6 to 6
Outputs:
- activations: float32 [8192, 1536], P(('row', 'col'))
- tokens_grad: float32 [8192, 1536], P(('row', 'col'))
- norm_attn_grad: float32 [2, 1536], replicated
- qkv_weight_grad: float32 [2, 1536, 3072], P(None, 'row', 'col')
- out_weight_grad: float32 [2, 1536, 1536], P(None, 'col', 'row')
- norm_mlp_grad: float32 [2, 1536], replicated
- gate_up_grad: float32 [2, 1536, 2, 4096], P(None, 'row', None, 'col')
- down_grad: float32 [2, 1536, 4096], P(None, 'row', 'col')
The draws below stay inside these ranges and needn't reach their ends.
Inputs may be any that keep to these rules, and one draw needn't show every extreme that they name: `segment_ids`: segment ids never fall from one token to the next, no id spans two packs of 1024 tokens, each pack holds one to four documents, and some pack holds a single document. `positions`: A token's position counts the tokens of its document before it.
All inputs are finite; a program needn't handle non-finite values.
Results may differ from the reference program's by a relative error of at most 0.029.
Values may be sent and summed in bfloat16 or wider, within the bound.
No kernel may reach another device: no remote copies, remote signals or barrier semaphores. Data moves between devices by JAX's collectives and lax.ppermute only.
A program may use at most 256 MiB of HBM per device.

```python
import jax
import jax.numpy as jnp
from jax import lax

D = 1536
H = 16
KVH = 8
HD = 96
FF = 4096
LAYERS = 2
TOK_DEV = 1024
GROUP = 2
QKV = 3072
TOKENS = 8192


def doc_layout(key):
    packs = TOKENS // TOK_DEV
    token_index = jnp.arange(TOKENS, dtype=jnp.int32)
    in_pack = token_index % TOK_DEV
    pack_of = token_index // TOK_DEV
    spread = TOK_DEV // 8
    moves = jax.random.randint(jax.random.fold_in(key, 11), (packs, 3), -spread, spread + 1).astype(jnp.int32)
    centres = (jnp.arange(1, 4, dtype=jnp.int32) * (TOK_DEV // 4))[None, :]
    bounds = centres + moves
    whole_pack = jax.random.randint(jax.random.fold_in(key, 12), (), 0, packs - 1).astype(jnp.int32)
    is_whole = (jnp.arange(packs, dtype=jnp.int32) == whole_pack)[:, None]
    bounds = jnp.where(is_whole, jnp.int32(TOK_DEV), bounds).astype(jnp.int32)
    mine = bounds[pack_of]
    passed = in_pack[:, None] >= mine
    local_id = jnp.sum(passed.astype(jnp.int32), axis=1)
    seg_begin = jnp.max(jnp.where(passed, mine, 0), axis=1)
    seg_ids = pack_of * 4 + local_id
    return (seg_ids.astype(jnp.int32), (in_pack - seg_begin).astype(jnp.int32))


def draw_segment_ids(key, part):
    return doc_layout(key)[0]


def draw_positions(key, part):
    return doc_layout(key)[1]


def shard_levels(key, shape, pieces, least, largest):
    factor_of, own = 1.0, jax.random.fold_in(key, 6)
    for dim, blocks in pieces:
        draws = jnp.exp(jax.random.uniform(jax.random.fold_in(own, dim), (blocks,), jnp.float32, least / len(pieces), largest / len(pieces)))
        factor_of = factor_of * jnp.repeat(draws, shape[dim] // blocks).reshape([-1 if axis == dim else 1 for axis in range(len(shape))])
    return factor_of


def noise(rng, dims, scale, limit, pieces=(), kind=jnp.bfloat16):
    values = jax.random.normal(rng, dims, jnp.float32) * scale
    if len(pieces) > 0:
        values = shard_levels(rng, dims, pieces, -0.22, 0.18) * values
    return jnp.clip(values, min=-limit, max=limit).astype(kind)


def setup_inputs(seed: int = 0) -> dict:
    keys = jax.random.split(jax.random.key(seed), 11)
    tokens = noise(keys[0], (TOKENS, D), 1.0, 6.0, ((0, 32),))
    segment_ids = draw_segment_ids(jax.random.fold_in(keys[10], 71), 0)
    positions = draw_positions(jax.random.fold_in(keys[10], 71), 0)
    norm_attn = jnp.clip(1.0 + 0.1 * jax.random.normal(keys[3], (LAYERS, D), jnp.float32), 0.5, 1.5)
    qkv_weight = noise(keys[4], (LAYERS, D, QKV), D ** -0.5, 0.15625, ((1, 8), (2, 4)))
    out_weight = noise(keys[5], (LAYERS, H * HD, D), (H * HD // 16) ** -0.5, 0.625, ((1, 4), (2, 8)))
    norm_mlp = jnp.clip(1.0 + 0.1 * jax.random.normal(keys[6], (LAYERS, D), jnp.float32), 0.5, 1.5)
    gate_up_weight = noise(keys[7], (LAYERS, D, 2, FF), D ** -0.5, 0.15625, ((1, 8), (3, 4)))
    down_weight = noise(keys[8], (LAYERS, D, FF), FF ** -0.5, 0.09375, ((1, 8), (2, 4)))
    cotangent = noise(keys[9], (TOKENS, D), 1.0, 6.0, ((0, 32),))
    return {"tokens": tokens, "segment_ids": segment_ids, "positions": positions, "norm_attn": norm_attn, "qkv_weight": qkv_weight, "out_weight": out_weight, "norm_mlp": norm_mlp, "gate_up_weight": gate_up_weight, "down_weight": down_weight, "cotangent": cotangent}


EPS = 1e-05
THETA = 100000.0
PRECISE = lax.Precision.HIGHEST

@jax.custom_vjp
def low(v):
    return lax.optimization_barrier(v.astype(jnp.bfloat16)).astype(jnp.float32)

@jax.custom_vjp
def low_back(v):
    return v

def low_keep(v):
    return (low(v), None)

def low_pass(kept, grad):
    return (grad,)

def back_keep(v):
    return (v, None)

def back_low(kept, grad):
    return (low(grad),)
low.defvjp(low_keep, low_pass)
low_back.defvjp(back_keep, back_low)

def rope_tables(positions):
    half_dim = HD // 2
    inv_freq = THETA ** (-(jnp.arange(half_dim, dtype=jnp.float32) * 2.0 / HD))
    angles = positions.astype(jnp.float32)[:, None] * inv_freq[None, :]
    cosine = jnp.concatenate([jnp.cos(angles), jnp.cos(angles)], axis=1)
    sine_tab = jnp.concatenate([jnp.sin(angles), jnp.sin(angles)], axis=1)
    return (cosine, sine_tab)

def rotate(values_in, cosine, sine_tab):
    half_dim = HD // 2
    turned = jnp.concatenate([-values_in[..., half_dim:], values_in[..., :half_dim]], axis=-1)
    return values_in * cosine + turned * sine_tab

def normalize(resid, gain):
    inv_rms = lax.rsqrt(lax.optimization_barrier(jnp.mean(resid * resid, axis=1, keepdims=True)) + EPS)
    return resid * inv_rms * gain

def attend_pack(block_args):
    query, key_rows, values_in, seg_ids = block_args
    scores = jnp.einsum('qjgd,kjd->jgqk', query, key_rows, precision=PRECISE) * HD ** (-0.5)
    scores = low_back(scores)
    offsets = jnp.arange(TOK_DEV)
    allowed = (seg_ids[:, None] == seg_ids[None, :]) & (offsets[:, None] >= offsets[None, :])
    scores = jnp.where(allowed, scores, -1e+30)
    row_max = lax.optimization_barrier(jnp.max(scores, axis=-1, keepdims=True))
    expo = jnp.exp(scores - row_max)
    probs = low(expo / lax.optimization_barrier(jnp.sum(expo, axis=-1, keepdims=True)))
    return jnp.einsum('jgqk,kjd->qjgd', probs, values_in, precision=PRECISE)

def layer_forward(resid, gain_attn, w_qkv, w_out, gain_mlp, w_gu, w_down, segment_ids, cosine, sine_tab):
    packs = TOKENS // TOK_DEV
    normed = low(normalize(resid, gain_attn))
    mixed = low_back(jnp.dot(normed, w_qkv, precision=PRECISE)).reshape(TOKENS, KVH, GROUP + 2, HD)
    query = low(rotate(mixed[:, :, :GROUP], cosine[:, None, None, :], sine_tab[:, None, None, :]))
    key_rows = low(rotate(mixed[:, :, GROUP], cosine[:, None, :], sine_tab[:, None, :]))
    values_in = low(mixed[:, :, GROUP + 1])
    attended = lax.map(jax.checkpoint(attend_pack), (query.reshape(packs, TOK_DEV, KVH, GROUP, HD), key_rows.reshape(packs, TOK_DEV, KVH, HD), values_in.reshape(packs, TOK_DEV, KVH, HD), segment_ids.reshape(packs, TOK_DEV)))
    attended = low_back(low(attended.reshape(TOKENS, H * HD)))
    middle = resid + low_back(jnp.dot(attended, w_out, precision=PRECISE))
    normed_mlp = low(normalize(middle, gain_mlp))
    gate_up = low_back(jnp.einsum('td,dcf->tcf', normed_mlp, w_gu, precision=PRECISE))
    hidden = low(jax.nn.silu(gate_up[:, 0]) * gate_up[:, 1])
    return middle + low_back(jnp.einsum('tf,df->td', hidden, w_down, precision=PRECISE))

def reference(tokens, segment_ids, positions, norm_attn, qkv_weight, out_weight, norm_mlp, gate_up_weight, down_weight, cotangent):
    cosine, sine_tab = rope_tables(positions)
    weights_all = (norm_attn, qkv_weight.astype(jnp.float32), out_weight.astype(jnp.float32), norm_mlp, gate_up_weight.astype(jnp.float32), down_weight.astype(jnp.float32))

    def forward(resid, weights_all):
        gains_a, w_qkvs, w_outs, gains_m, w_gus, w_downs = weights_all
        for layer_index in range(LAYERS):
            resid = layer_forward(resid, gains_a[layer_index], w_qkvs[layer_index], w_outs[layer_index], gains_m[layer_index], w_gus[layer_index], w_downs[layer_index], segment_ids, cosine, sine_tab)
        return resid
    result, pull_back = jax.vjp(forward, tokens.astype(jnp.float32), weights_all)
    grad_tokens, grad_weights = pull_back(cotangent.astype(jnp.float32))
    return (result, grad_tokens, grad_weights[0], grad_weights[1], grad_weights[2], grad_weights[3], grad_weights[4], grad_weights[5])
```

```python
import jax
import jax.numpy as jnp
from jax import lax
from jax.sharding import PartitionSpec as P

HD = 96
GROUP = 2
EPS = 1e-05
THETA = 100000.0
F32 = jnp.float32
BF16 = jnp.bfloat16


def rope_tables(positions):
    half_dim = HD // 2
    inv_freq = THETA ** (-(jnp.arange(half_dim, dtype=F32) * 2.0 / HD))
    angles = positions.astype(F32)[:, None] * inv_freq[None, :]
    cosine = jnp.cos(angles)
    sine = jnp.sin(angles)
    return jnp.concatenate([cosine, cosine], axis=1), jnp.concatenate([sine, sine], axis=1)


def rotate(u, cosine, sine):
    half_dim = HD // 2
    turned = jnp.concatenate([-u[..., half_dim:], u[..., :half_dim]], axis=-1)
    return u * cosine + turned * sine


def rotate_back(u, cosine, sine):
    half_dim = HD // 2
    turned = u * sine
    return u * cosine + jnp.concatenate([turned[..., half_dim:], -turned[..., :half_dim]], axis=-1)


def norm_scale(resid, gain):
    inv_rms = lax.rsqrt(jnp.mean(resid * resid, axis=1) + EPS)
    return (resid * inv_rms[:, None] * gain).astype(BF16), inv_rms


def norm_back(resid, inv_rms, gain, grad_normed):
    width = resid.shape[1]
    weighted = grad_normed * gain
    inner = jnp.sum(weighted * resid, axis=1)
    grad_resid = inv_rms[:, None] * weighted - resid * (inv_rms**3 * inner / width)[:, None]
    grad_gain = jnp.sum(grad_normed * resid * inv_rms[:, None], axis=0)
    return grad_resid, grad_gain


class Grid:
    def __init__(self, rows, cols):
        self.rows, self.cols = rows, cols
        self.chips, self.parts = rows // 2, cols // 2
        row, col = lax.axis_index("row"), lax.axis_index("col")
        self.core, self.chip = row % 2, row // 2
        self.pair, self.part = col % 2, col // 2

    def row_swap(self, value, mask):
        return lax.ppermute(value, "row", [(r, r ^ mask) for r in range(self.rows)])

    def swap_core(self, value):
        return self.row_swap(value, 1)

    def swap_chip(self, value, mask):
        return self.row_swap(value, 2 * mask)

    def swap_pair(self, value):
        return lax.ppermute(value, "col", [(c, c ^ 1) for c in range(self.cols)])

    def swap_part(self, value):
        return lax.ppermute(value, "col", [(c, c ^ 2) for c in range(self.cols)])

    def send_part(self, value, offset, upward):
        moves = []
        for c in range(self.cols):
            other = c ^ (2 * offset)
            if (other > c) == upward:
                moves.append((c, other))
        return lax.ppermute(value, "col", moves)

    def part_groups(self):
        return [[2 * p + q for p in range(self.parts)] for q in range(2)]

    def chip_blocks(self, value, axis):
        size = value.shape[axis] // self.chips
        return jnp.concatenate(
            [
                lax.dynamic_slice_in_dim(value, (self.chip ^ j) * size, size, axis)
                for j in range(self.chips)
            ],
            axis=axis,
        )


def halves(value, axis):
    size = value.shape[axis] // 2
    return (
        lax.slice_in_dim(value, 0, size, axis=axis),
        lax.slice_in_dim(value, size, 2 * size, axis=axis),
    )


def gather_chips(grid, own, axis):
    if grid.chips == 4:
        first = grid.swap_chip(own, 1)
        second = grid.swap_chip(own, 2)
        far_a = grid.swap_chip(halves(first, axis)[0], 2)
        far_b = grid.swap_chip(halves(second, axis)[1], 1)
        return [own, first, second, jnp.concatenate([far_a, far_b], axis=axis)]
    blocks = [own]
    mask = 1
    while mask < grid.chips:
        blocks = blocks + [grid.swap_chip(b, mask) for b in blocks]
        mask *= 2
    return blocks


def scatter_chips(grid, blocks, axis):
    if grid.chips == 4:
        own, first, second, far = blocks
        far_a, far_b = halves(far, axis)
        got_a = grid.swap_chip(far_a, 2)
        got_b = grid.swap_chip(far_b, 1)
        f_a, f_b = halves(first, axis)
        s_a, s_b = halves(second, axis)
        f_a = (f_a.astype(F32) + got_a.astype(F32)).astype(BF16)
        s_b = (s_b.astype(F32) + got_b.astype(F32)).astype(BF16)
        got_first = grid.swap_chip(jnp.concatenate([f_a, f_b], axis=axis), 1)
        got_second = grid.swap_chip(jnp.concatenate([s_a, s_b], axis=axis), 2)
        total = own.astype(F32) + got_first.astype(F32) + got_second.astype(F32)
        return total.astype(BF16)
    mask = grid.chips // 2
    while mask >= 1:
        got = [grid.swap_chip(b, mask) for b in blocks[mask:]]
        blocks = [
            (b.astype(F32) + g.astype(F32)).astype(BF16) for b, g in zip(blocks[:mask], got)
        ]
        mask //= 2
    return blocks[0]


def gather_weight(grid, shard, wide, cut):
    mine = grid.core == 0
    if grid.parts == 2:
        other = grid.swap_part(shard)
        straight = grid.part == grid.core
        keep = jnp.where(straight, shard, other)
        send = jnp.where(straight, other, shard)
    else:
        every = lax.all_gather(shard, "col", axis_index_groups=grid.part_groups())
        even = jnp.concatenate([every[i] for i in range(0, grid.parts, 2)], axis=cut)
        odd = jnp.concatenate([every[i] for i in range(1, grid.parts, 2)], axis=cut)
        keep = jnp.where(mine, even, odd)
        send = jnp.where(mine, odd, even)
    got = grid.swap_core(send)
    own = jnp.concatenate([jnp.where(mine, keep, got), jnp.where(mine, got, keep)], axis=wide)
    return jnp.concatenate(gather_chips(grid, own, wide), axis=wide)


def scatter_weight(grid, partial, wide, cut):
    mine = grid.core == 0
    size = partial.shape[wide] // grid.chips
    blocks = [
        lax.slice_in_dim(partial, j * size, (j + 1) * size, axis=wide) for j in range(grid.chips)
    ]
    total = scatter_chips(grid, blocks, wide)
    low, high = halves(total, wide)
    keep = jnp.where(mine, low, high)
    got = grid.swap_core(jnp.where(mine, high, low))
    if grid.parts == 2:
        straight = grid.part == grid.core
        own = jnp.where(straight, keep, got)
        back = grid.swap_part(jnp.where(straight, got, keep))
        return own.astype(F32) + back.astype(F32)
    even = jnp.where(mine, keep, got)
    odd = jnp.where(mine, got, keep)
    count = grid.parts // 2
    width = even.shape[cut] // count
    every = []
    for i in range(count):
        for source in (even, odd):
            every.append(lax.slice_in_dim(source, i * width, (i + 1) * width, axis=cut))
    return lax.psum_scatter(
        jnp.stack(every), "col", scatter_dimension=0, axis_index_groups=grid.part_groups()
    ).astype(F32)


def gather_tokens(grid, rows):
    both = jnp.concatenate([rows, grid.swap_pair(rows)], axis=0)
    return jnp.concatenate([both, grid.swap_core(both)], axis=0)


def sum_tokens(grid, partial):
    count = partial.shape[0] // 2
    got = grid.swap_core(partial[count:].astype(BF16))
    both = partial[:count].astype(F32) + got.astype(F32)
    quarter = count // 2
    got = grid.swap_pair(both[quarter:].astype(BF16))
    return both[:quarter] + got.astype(F32)


def part_tokens(grid, values, index, tok):
    part = grid.part ^ index
    return jnp.concatenate(
        [
            lax.dynamic_slice_in_dim(values, (2 * part + grid.pair) * tok, tok, 0),
            lax.dynamic_slice_in_dim(values, (2 * part + 1 - grid.pair) * tok, tok, 0),
        ]
    )


def attention_forward(query, keys, values, allowed):
    scores = (
        jnp.einsum("bqjgd,bkjd->bjgqk", query, keys, preferred_element_type=F32) * HD**-0.5
    )
    scores = jnp.where(allowed[:, None, None], scores, -1e30)
    row_max = jnp.max(scores, axis=-1, keepdims=True)
    expo = jnp.exp(scores - row_max)
    total = jnp.sum(expo, axis=-1, keepdims=True)
    probs = (expo / total).astype(BF16)
    attended = jnp.einsum("bjgqk,bkjd->bqjgd", probs, values, preferred_element_type=F32)
    return attended, row_max + jnp.log(total)


def attention_backward(query, keys, values, allowed, log_total, grad_att):
    scores = (
        jnp.einsum("bqjgd,bkjd->bjgqk", query, keys, preferred_element_type=F32) * HD**-0.5
    )
    probs = jnp.where(allowed[:, None, None], jnp.exp(scores - log_total), 0.0)
    grad_values = jnp.einsum(
        "bjgqk,bqjgd->bkjd", probs.astype(BF16), grad_att, preferred_element_type=F32
    )
    grad_probs = jnp.einsum("bqjgd,bkjd->bjgqk", grad_att, values, preferred_element_type=F32)
    delta = jnp.sum(grad_probs * probs, axis=-1, keepdims=True)
    grad_scores = (probs * (grad_probs - delta)).astype(BF16)
    grad_query = (
        jnp.einsum("bjgqk,bkjd->bqjgd", grad_scores, keys, preferred_element_type=F32) * HD**-0.5
    )
    grad_keys = (
        jnp.einsum("bjgqk,bqjgd->bkjd", grad_scores, query, preferred_element_type=F32)
        * HD**-0.5
    )
    return grad_query, grad_keys, grad_values


def per_device(
    rows,
    cols,
    tokens,
    segment_ids,
    positions,
    norm_attn,
    qkv_weight,
    out_weight,
    norm_mlp,
    gate_up_weight,
    down_weight,
    cotangent,
):
    grid = Grid(rows, cols)
    layers = qkv_weight.shape[0]
    tok = tokens.shape[0]
    span = 2 * tok
    parts = grid.parts
    other_seg = grid.swap_core(segment_ids)
    other_pos = grid.swap_core(positions)
    packs_seg, packs_pos = (segment_ids, other_seg), (positions, other_pos)
    local_pos = jnp.concatenate([part_tokens(grid, v, 0, tok) for v in packs_pos])
    cosine, sine = rope_tables(local_pos)
    cosine = cosine.reshape(2, span, 1, HD)
    sine = sine.reshape(2, span, 1, HD)
    seg_q = jnp.stack([part_tokens(grid, v, 0, tok) for v in packs_seg])
    seg_k = jnp.stack(
        [
            jnp.concatenate([part_tokens(grid, v, j, tok) for j in range(parts)])
            for v in packs_seg
        ]
    )
    place = jnp.arange(segment_ids.shape[0])
    place_q = part_tokens(grid, place, 0, tok)
    place_k = jnp.concatenate([part_tokens(grid, place, j, tok) for j in range(parts)])
    allowed = (seg_q[:, :, None] == seg_k[:, None, :]) & (
        place_q[None, :, None] >= place_k[None, None, :]
    )

    gains_a = grid.chip_blocks(norm_attn, 1)
    gains_m = grid.chip_blocks(norm_mlp, 1)
    resid = grid.chip_blocks(tokens, 1).astype(F32)

    def all_keys(local):
        blocks = [local] + [grid.send_part(local, j, True) for j in range(1, parts)]
        return jnp.concatenate(blocks, axis=1)

    def own_keys(every):
        blocks = jnp.split(every, parts, axis=1)
        total = blocks[0]
        for j in range(1, parts):
            total = total + grid.send_part(blocks[j].astype(BF16), j, False).astype(F32)
        return total

    saved = []
    for l in range(layers):
        w_qkv = gather_weight(grid, qkv_weight[l], 0, 1)
        w_out = gather_weight(grid, out_weight[l], 1, 0)
        w_gu = gather_weight(grid, gate_up_weight[l], 0, 2)
        w_down = gather_weight(grid, down_weight[l], 0, 1)
        groups = w_qkv.shape[1] // ((GROUP + 2) * HD)
        own_normed, inv_rms = norm_scale(resid, gains_a[l])
        normed = gather_tokens(grid, own_normed)
        mixed = jnp.dot(normed, w_qkv, preferred_element_type=F32).reshape(
            2, span, groups, GROUP + 2, HD
        )
        query = rotate(mixed[:, :, :, :GROUP], cosine[:, :, None], sine[:, :, None]).astype(BF16)
        keys = rotate(mixed[:, :, :, GROUP], cosine, sine).astype(BF16)
        values = mixed[:, :, :, GROUP + 1].astype(BF16)
        keys, values = all_keys(keys), all_keys(values)
        attended, log_total = attention_forward(query, keys, values, allowed)
        attended = attended.reshape(2 * span, groups * GROUP * HD).astype(BF16)
        middle = resid + sum_tokens(
            grid, jnp.dot(attended, w_out, preferred_element_type=F32)
        )
        own_normed, inv_rms_mlp = norm_scale(middle, gains_m[l])
        normed_mlp = gather_tokens(grid, own_normed)
        gate_up = jnp.einsum("td,dcf->tcf", normed_mlp, w_gu, preferred_element_type=F32)
        hidden = (jax.nn.silu(gate_up[:, 0]) * gate_up[:, 1]).astype(BF16)
        saved.append(
            (
                (resid, inv_rms, middle, inv_rms_mlp),
                (normed, query, keys, values, log_total, attended, normed_mlp, gate_up, hidden),
                (w_qkv, w_out, w_gu, w_down),
            )
        )
        resid = middle + sum_tokens(
            grid, jnp.einsum("tf,df->td", hidden, w_down, preferred_element_type=F32)
        )

    grad_resid = grid.chip_blocks(cotangent, 1).astype(F32)
    grads = [None] * layers
    gain_grads = [None] * layers
    for l in reversed(range(layers)):
        resid_in, inv_rms, middle, inv_rms_mlp = saved[l][0]
        normed, query, keys, values, log_total, attended, normed_mlp, gate_up, hidden = saved[l][1]
        w_qkv, w_out, w_gu, w_down = saved[l][2]
        groups = w_qkv.shape[1] // ((GROUP + 2) * HD)
        grad_full = gather_tokens(grid, grad_resid.astype(BF16))
        grad_w_down = jnp.einsum("td,tf->df", grad_full, hidden, preferred_element_type=F32)
        grad_hidden = jnp.einsum("td,df->tf", grad_full, w_down, preferred_element_type=F32)
        gate, up = gate_up[:, 0], gate_up[:, 1]
        sigma = jax.nn.sigmoid(gate)
        grad_gate = grad_hidden * up * sigma * (1.0 + gate * (1.0 - sigma))
        grad_up = grad_hidden * gate * sigma
        grad_gu = jnp.stack([grad_gate, grad_up], axis=1).astype(BF16)
        grad_w_gu = jnp.einsum("td,tcf->dcf", normed_mlp, grad_gu, preferred_element_type=F32)
        grad_nm = sum_tokens(
            grid, jnp.einsum("tcf,dcf->td", grad_gu, w_gu, preferred_element_type=F32)
        )
        grad_norm, gain_m = norm_back(middle, inv_rms_mlp, gains_m[l], grad_nm)
        grad_mid = grad_resid + grad_norm
        grad_full = gather_tokens(grid, grad_mid.astype(BF16))
        grad_w_out = jnp.einsum("th,td->hd", attended, grad_full, preferred_element_type=F32)
        grad_att = jnp.einsum("td,hd->th", grad_full, w_out, preferred_element_type=F32)
        grad_att = grad_att.astype(BF16).reshape(2, span, groups, GROUP, HD)
        grad_query, grad_keys, grad_values = attention_backward(
            query, keys, values, allowed, log_total, grad_att
        )
        grad_keys, grad_values = own_keys(grad_keys), own_keys(grad_values)
        grad_query = rotate_back(grad_query, cosine[:, :, None], sine[:, :, None])
        grad_keys = rotate_back(grad_keys, cosine, sine)
        grad_mixed = jnp.concatenate(
            [grad_query, grad_keys[:, :, :, None], grad_values[:, :, :, None]], axis=3
        )
        grad_mixed = grad_mixed.reshape(2 * span, groups * (GROUP + 2) * HD).astype(BF16)
        grad_w_qkv = jnp.einsum("td,tc->dc", normed, grad_mixed, preferred_element_type=F32)
        grad_na = sum_tokens(
            grid, jnp.einsum("tc,dc->td", grad_mixed, w_qkv, preferred_element_type=F32)
        )
        grad_norm, gain_a = norm_back(resid_in, inv_rms, gains_a[l], grad_na)
        grad_resid = grad_mid + grad_norm
        grads[l] = (
            scatter_weight(grid, grad_w_qkv.astype(BF16), 0, 1),
            scatter_weight(grid, grad_w_out.astype(BF16), 1, 0),
            scatter_weight(grid, grad_w_gu.astype(BF16), 0, 2),
            scatter_weight(grid, grad_w_down.astype(BF16), 0, 1),
        )
        gain_grads[l] = (gain_a, gain_m)
    gain_all = jnp.stack([g for pair in gain_grads for g in pair])
    gain_all = lax.psum(grid.chip_blocks(gain_all, 1), ("row", "col"))
    return (
        grid.chip_blocks(resid, 1),
        grid.chip_blocks(grad_resid, 1),
        gain_all[0::2],
        jnp.stack([g[0] for g in grads]),
        jnp.stack([g[1] for g in grads]),
        gain_all[1::2],
        jnp.stack([g[2] for g in grads]),
        jnp.stack([g[3] for g in grads]),
    )


def solution(mesh):
    rows, cols = mesh.shape["row"], mesh.shape["col"]
    in_specs = (
        P(("row", "col"), None),
        P("row"),
        P("row"),
        P(),
        P(None, "row", "col"),
        P(None, "col", "row"),
        P(),
        P(None, "row", None, "col"),
        P(None, "row", "col"),
        P(("row", "col"), None),
    )
    out_specs = (
        P(("row", "col"), None),
        P(("row", "col"), None),
        P(),
        P(None, "row", "col"),
        P(None, "col", "row"),
        P(),
        P(None, "row", None, "col"),
        P(None, "row", "col"),
    )

    def step(*args):
        return per_device(rows, cols, *args)

    return jax.shard_map(step, mesh=mesh, in_specs=in_specs, out_specs=out_specs, check_vma=False)
```
